32 devices in a mesh: px: 8 (over z, y), py: 4 (over x, core).
Axes of the slice: x: 2, y: 2, z: 4, core: 2. Of those that a mesh axis runs over, the one named last changes fastest.
Arguments:
- spectrum: float32 [2, 1536, 24576], P(None, 'px', 'py'), may hold values from -6 to 6
- concentration: float32 [3072, 24576], P('px', 'py'), may hold values from -6 to 6
- factor_y: float32 [1536, 128], P('py'), may hold values from -0.15625 to 0.15625
- factor_x: float32 [3072, 256], P('px'), may hold values from -0.109375 to 0.109375
Outputs:
- y_compressed: float32 [16, 3072, 128], P('py', 'px')
- core_tensor: float32 [16, 256, 128], P('py', 'px')
The draws below stay inside these ranges and needn't reach their ends.
All inputs are finite; a program needn't handle non-finite values.
Results may differ from the reference program's by a relative error of at most 0.000076.
Values sent between devices are 32-bit elements; how exact they have to be, the bound alone decides.
No kernel may reach another device: no remote copies, remote signals or barrier semaphores. Data moves between devices by JAX's collectives and lax.ppermute only.
A program may use at most 128 MiB of HBM per device.

```python
import math
import jax
import jax.numpy as jnp
from jax import lax

NX = 3072
NY = 1536
RX = 256
RY = 128
NZ = 16
KX = 1536


def block_levels(rng, extent, pieces, low, high):
    level = 1.0
    for dim, blocks in pieces:
        steps = jax.random.uniform(jax.random.fold_in(jax.random.fold_in(rng, 6), dim), (blocks,), jnp.float32, low / len(pieces), high / len(pieces))
        level = level * jnp.repeat(jnp.exp(steps), extent[dim] // blocks).reshape((-1,) + (1,) * (len(extent) - 1 - dim))
    return level


def noise(key, dims, deviation, most, shards=(), dtype=jnp.bfloat16):
    result = jax.random.normal(key, dims, jnp.float32) * deviation
    if len(shards) > 0:
        result = block_levels(key, dims, shards, -0.22, 0.18) * result
    return jnp.clip(result, min=-most, max=most).astype(dtype)


def setup_inputs(seed: int = 0) -> dict:
    keys = jax.random.split(jax.random.key(seed), 5)
    return {
        "spectrum": noise(keys[0], (2, KX, NY * NZ), 1.0, 6.0, ((1, 8), (2, 4)), jnp.float32),
        "concentration": noise(keys[1], (NX, NY * NZ), 1.0, 6.0, ((0, 8), (1, 4)), jnp.float32),
        "factor_y": noise(keys[2], (NY, RY), NY ** -0.5, 0.15625, ((0, 4),), jnp.float32),
        "factor_x": noise(keys[3], (NX, RX), NX ** -0.5, 0.109375, ((0, 8),), jnp.float32),
    }


def reference(spectrum, concentration, factor_y, factor_x):
    modes = spectrum.reshape(2, KX, NY, NZ)
    complex_modes = lax.complex(modes[0], modes[1])
    padded = jnp.concatenate([complex_modes, jnp.zeros_like(complex_modes[:1])], axis=0)
    velocity = jnp.fft.irfft(padded, n=NX, axis=0) * (NX / math.sqrt(KX))
    flux = velocity * concentration.reshape(NX, NY, NZ)
    y_compressed = jnp.einsum('xyz,yr->zxr', flux, factor_y, precision=lax.Precision.HIGHEST)
    core_tensor = jnp.einsum('xs,zxr->zsr', factor_x, y_compressed, precision=lax.Precision.HIGHEST)
    return (y_compressed, core_tensor)
```

```python
import functools
import math

import jax
import jax.numpy as jnp
from jax import lax
from jax.experimental import pallas as pl
from jax.experimental.pallas import tpu as pltpu
from jax.sharding import PartitionSpec as P

HIGHEST = lax.Precision.HIGHEST
LANES = 128


def exchange(value, axis, size, offset):
    return lax.ppermute(value, axis, [(a, a ^ offset) for a in range(size)])


def synth_table(grid, modes, first_x, block_width):
    wave = lax.broadcasted_iota(jnp.int32, (modes, block_width), 0)
    column = first_x + lax.broadcasted_iota(jnp.int32, (modes, block_width), 1)
    phase = wave * column % grid
    angle = phase.astype(jnp.float32) * (2.0 * math.pi / grid)
    weight = jnp.where(wave == 0, 1.0, 2.0) / math.sqrt(modes)
    return jnp.concatenate([weight * jnp.cos(angle), -weight * jnp.sin(angle)], axis=0)


def general_body(px, spectrum, concentration, factor_y, factor_x):
    x_local, line_total = concentration.shape
    y_local = factor_y.shape[0]
    grid, modes = x_local * px, spectrum.shape[1] * px
    pencil = lax.all_to_all(spectrum, "px", split_axis=2, concat_axis=1, tiled=True)
    lines = pencil.shape[2]
    stacked = pencil.reshape(2 * modes, lines)

    def fill(block, velocity):
        rows = lax.dot_general(
            synth_table(grid, modes, block * x_local, x_local),
            stacked,
            (((0,), (0,)), ((), ())),
            precision=HIGHEST,
            preferred_element_type=jnp.float32,
        )
        return lax.dynamic_update_slice_in_dim(velocity, rows, block * x_local, 0)

    velocity = lax.fori_loop(0, px, fill, jnp.zeros((grid, lines), jnp.float32))
    returned = lax.all_to_all(velocity, "px", split_axis=0, concat_axis=1, tiled=True)
    flux = (returned * concentration).reshape(x_local, y_local, line_total // y_local)
    y_compressed = lax.psum_scatter(
        jnp.einsum("xyz,yr->zxr", flux, factor_y, precision=HIGHEST),
        "py",
        scatter_dimension=0,
        tiled=True,
    )
    terms = jnp.einsum("xs,zxr->zsr", factor_x, y_compressed, precision=HIGHEST)
    return y_compressed, lax.psum_scatter(terms, "px", scatter_dimension=1, tiled=True)


def pack_kernel(planes, groups, blocks_ref, in_ref, *refs):
    outs, turned = refs[:-1], refs[-1]
    turned[...] = in_ref[...].T
    stride = turned.shape[0] // outs[0].shape[-2] * len(groups[0])
    count = turned.shape[0] // planes
    sets = sum(len(g) for g in groups)
    for out, group in zip(outs, groups):
        row = 0
        for j in group:
            for zb in range(planes // sets):
                part = turned[pl.ds(zb * sets + j, count, stride=planes), :]
                if len(out.shape) == 3:
                    out[0, row : row + count, :] = part
                else:
                    out[row : row + count, :] = part
                row += count


def pack_peer(value, block, width, planes, groups):
    rows = value.shape[0]
    sets = sum(len(g) for g in groups)
    shapes = [(width // sets * len(g), rows) for g in groups]
    return pl.pallas_call(
        functools.partial(pack_kernel, planes, groups),
        out_shape=[jax.ShapeDtypeStruct(s, value.dtype) for s in shapes],
        grid_spec=pltpu.PrefetchScalarGridSpec(
            num_scalar_prefetch=1,
            grid=(rows // LANES,),
            in_specs=[pl.BlockSpec((LANES, width), lambda i, b: (i, b[0]))],
            out_specs=[pl.BlockSpec((s[0], LANES), lambda i, b: (0, i)) for s in shapes],
            scratch_shapes=[pltpu.VMEM((width, LANES), value.dtype)],
        ),
        cost_estimate=pl.CostEstimate(flops=0, bytes_accessed=8 * rows * width, transcendentals=0),
        name="pack_peer",
    )(block, value)


def pack_all(value, blocks, width, planes, groups):
    rows, peers = value.shape[0], blocks.shape[0]
    sets = sum(len(g) for g in groups)
    shapes = [(peers, width // sets * len(g), rows) for g in groups]
    return pl.pallas_call(
        functools.partial(pack_kernel, planes, groups),
        out_shape=[jax.ShapeDtypeStruct(s, value.dtype) for s in shapes],
        grid_spec=pltpu.PrefetchScalarGridSpec(
            num_scalar_prefetch=1,
            grid=(peers, rows // LANES),
            in_specs=[pl.BlockSpec((LANES, width), lambda s, i, b: (i, b[s]))],
            out_specs=[pl.BlockSpec((1, s[1], LANES), lambda s, i, b: (s, 0, i)) for s in shapes],
            scratch_shapes=[pltpu.VMEM((width, LANES), value.dtype)],
        ),
        cost_estimate=pl.CostEstimate(
            flops=0, bytes_accessed=8 * rows * width * peers, transcendentals=0
        ),
        name="pack_all",
    )(blocks, value)


def table_kernel(cos_far, sin_far, cos_near, sin_near, out):
    k_local, tiles = cos_far.shape[1], cos_far.shape[2]

    @pl.loop(0, k_local // 8)
    def _(step):
        row = pl.multiple_of(step * 8, 8)
        far_c, far_s = cos_far[0, pl.ds(row, 8), :], sin_far[0, pl.ds(row, 8), :]
        near_c, near_s = cos_near[0, pl.ds(row, 8), :], sin_near[0, pl.ds(row, 8), :]
        for u in range(tiles):
            c, s = far_c[:, u : u + 1], far_s[:, u : u + 1]
            lanes = slice(u * LANES, (u + 1) * LANES)
            out[pl.ds(row, 8), lanes] = c * near_c - s * near_s
            out[pl.ds(pl.multiple_of(k_local + row, 8), 8), lanes] = -(s * near_c + c * near_s)


def build_table(blocks, k_local, x_local):
    peers = blocks.shape[0]
    grid, modes = x_local * peers, k_local * peers
    wave = blocks[:, None] * k_local + jnp.arange(k_local, dtype=jnp.int32)[None, :]
    starts = jnp.arange(x_local // LANES, dtype=jnp.int32) * LANES
    far = (blocks[:, None] * x_local + starts[None, :]).reshape(-1)
    near = jnp.arange(LANES, dtype=jnp.int32)

    def angle(column):
        phase = wave[:, :, None] * column[None, None, :] % grid
        return phase.astype(jnp.float32) * (2.0 * math.pi / grid)

    weight = (jnp.where(wave == 0, 1.0, 2.0) / math.sqrt(modes)).astype(jnp.float32)[:, :, None]
    tables = (
        jnp.cos(angle(far)),
        jnp.sin(angle(far)),
        weight * jnp.cos(angle(near)),
        weight * jnp.sin(angle(near)),
    )
    size = 2 * k_local * peers * grid
    return pl.pallas_call(
        table_kernel,
        out_shape=jax.ShapeDtypeStruct((2 * modes, grid), jnp.float32),
        grid=(peers,),
        in_specs=[pl.BlockSpec((1,) + t.shape[1:], lambda s: (s, 0, 0)) for t in tables],
        out_specs=pl.BlockSpec((2 * k_local, grid), lambda s: (s, 0)),
        cost_estimate=pl.CostEstimate(flops=3 * size, bytes_accessed=4 * size, transcendentals=0),
        name="build_table",
    )(*tables)


def flux_kernel(peers, index_ref, *refs):
    v_refs, (c_ref, fy_ref, out, flux) = refs[:peers], refs[peers:]
    count = c_ref.shape[1]
    for s in range(peers):
        flux[s * count : (s + 1) * count, :] = v_refs[s][...] * c_ref[s]
    out[0] = jnp.dot(
        fy_ref[...], flux[...], precision=HIGHEST, preferred_element_type=jnp.float32
    )


def contract_flux(parts, place, conc, factor, me_y, owners):
    peers, rows, x_local = conc.shape
    count = rows // owners
    rank, y_local = factor.shape
    return pl.pallas_call(
        functools.partial(flux_kernel, peers),
        out_shape=jax.ShapeDtypeStruct((owners, rank, x_local), jnp.float32),
        grid_spec=pltpu.PrefetchScalarGridSpec(
            num_scalar_prefetch=1,
            grid=(owners,),
            in_specs=[
                pl.BlockSpec((count, x_local), lambda t, m: (place * owners + (m[0] ^ t), 0))
                for _ in parts
            ]
            + [
                pl.BlockSpec((peers, count, x_local), lambda t, m: (0, m[0] ^ t, 0)),
                pl.BlockSpec((rank, y_local), lambda t, m: (0, 0)),
            ],
            out_specs=pl.BlockSpec((1, rank, x_local), lambda t, m: (t, 0, 0)),
            scratch_shapes=[pltpu.VMEM((y_local, x_local), jnp.float32)],
        ),
        cost_estimate=pl.CostEstimate(
            flops=2 * owners * rank * y_local * x_local,
            bytes_accessed=8 * peers * rows * x_local,
            transcendentals=0,
        ),
        name="contract_flux",
    )(me_y, *parts, conc, factor)


def aligned_body(px, py, spectrum, concentration, factor_y, factor_x):
    k_local = spectrum.shape[1]
    x_local, line_total = concentration.shape
    y_local, rank = factor_y.shape
    planes = line_total // y_local
    sets = planes // py
    width = line_total // px
    y_peer = y_local // px
    me_x = lax.axis_index("px").astype(jnp.int32)
    me_y = lax.axis_index("py").astype(jnp.int32).reshape(1)
    blocks = me_x ^ jnp.arange(px, dtype=jnp.int32)
    half = px // 2
    order = [half]
    for i in range(1, half):
        order += [i, half + i]

    stacked = spectrum.reshape(2 * k_local, line_total)
    cut = max(1, sets // 2)
    out_groups = [g for g in (list(range(cut)), list(range(cut, sets))) if g]
    back_groups = [list(range(cut))] + [[j] for j in range(cut, sets)]

    packed = {s: pack_peer(stacked, blocks[s : s + 1], width, planes, out_groups) for s in order + [0]}
    arrived = []
    for g in range(len(out_groups)):
        got = {s: exchange(packed[s][g], "px", px, s) for s in order}
        got[0] = packed[0][g]
        arrived.append(got)

    table = build_table(blocks, k_local, x_local)
    conc = pack_all(concentration, blocks, width, planes, [[j] for j in range(sets)])
    factor = jnp.concatenate(
        [lax.dynamic_slice_in_dim(factor_y, blocks[s] * y_peer, y_peer, 0) for s in range(px)], axis=0
    ).T

    rows_set = y_peer * py
    velocity = {}
    for group, got in zip(out_groups, arrived):
        lines = jnp.concatenate([got[s] for s in range(px)], axis=1)
        whole = lax.dot_general(
            lines,
            table,
            (((1,), (0,)), ((), ())),
            precision=lax.Precision.HIGH,
            preferred_element_type=jnp.float32,
        )
        for at, j in enumerate(group):
            velocity[j] = (whole, at)

    y_parts, core_parts = [], []
    for group in back_groups:
        whole, first = velocity[group[0]]
        rows = slice(first * rows_set, (first + len(group)) * rows_set)
        own = whole[rows]
        parts = [None] * px
        parts[0] = own[:, :x_local]
        for s in order:
            parts[s] = exchange(own[:, s * x_local : (s + 1) * x_local], "px", px, s)
        cores = []
        for place, j in enumerate(group):
            sums = contract_flux(parts, place, conc[j], factor, me_y, py)
            total = sums[0]
            for t in range(1, py):
                total = total + exchange(sums[t], "py", py, t)
            y_parts.append(total.T)
            cores.append(
                lax.dot_general(
                    factor_x,
                    total,
                    (((0,), (1,)), ((), ())),
                    precision=HIGHEST,
                    preferred_element_type=jnp.float32,
                )
            )
        s_local = factor_x.shape[1] // px
        terms = jnp.stack(cores).reshape(len(group), px, s_local, rank).transpose(1, 0, 2, 3)
        terms = lax.all_to_all(terms, "px", split_axis=0, concat_axis=0, tiled=True)
        core_parts.append(jnp.sum(terms, axis=0))
    return jnp.stack(y_parts), jnp.concatenate(core_parts, axis=0)


def body(px, py, spectrum, concentration, factor_y, factor_x):
    x_local, line_total = concentration.shape
    y_local = factor_y.shape[0]
    planes = line_total // y_local
    aligned = (
        px > 1
        and px & (px - 1) == 0
        and py & (py - 1) == 0
        and planes % py == 0
        and planes % 8 == 0
        and (line_total // px) % LANES == 0
        and x_local % LANES == 0
        and y_local % (8 * px) == 0
        and spectrum.shape[1] * 2 == x_local
        and spectrum.shape[1] % 8 == 0
    )
    if aligned:
        return aligned_body(px, py, spectrum, concentration, factor_y, factor_x)
    return general_body(px, spectrum, concentration, factor_y, factor_x)


def solution(mesh):
    placed = (P(None, "px", "py"), P("px", "py"), P("py", None), P("px", None))
    return jax.shard_map(
        functools.partial(body, mesh.shape["px"], mesh.shape["py"]),
        mesh=mesh,
        in_specs=placed,
        out_specs=(P("py", "px", None), P("py", "px", None)),
        check_vma=False,
    )
```

```python
import functools
import math

import jax
import jax.numpy as jnp
from jax import lax
from jax.experimental import pallas as pl
from jax.experimental.pallas import tpu as pltpu
from jax.sharding import PartitionSpec as P


HIGHEST = lax.Precision.HIGHEST
LANES = 128


def exchange(value, axis, size, offset):
    return lax.ppermute(value, axis, [(a, a ^ offset) for a in range(size)])


def far_first(peers):
    half = peers // 2
    return list(range(half, peers)) + list(range(1, half))


def split_sets(sets):
    cut = max(1, sets // 2)
    out_groups = [g for g in (list(range(cut)), list(range(cut, sets))) if g]
    back_groups = [list(range(cut))] + [[j] for j in range(cut, sets)]
    return out_groups, back_groups


def synth_table(grid, modes, first_x, block_width):
    wave = lax.broadcasted_iota(jnp.int32, (modes, block_width), 0)
    column = first_x + lax.broadcasted_iota(jnp.int32, (modes, block_width), 1)
    phase = wave * column % grid
    angle = phase.astype(jnp.float32) * (2.0 * math.pi / grid)
    weight = jnp.where(wave == 0, 1.0, 2.0) / math.sqrt(modes)
    return jnp.concatenate([weight * jnp.cos(angle), -weight * jnp.sin(angle)], axis=0)


def general_body(px, spectrum, concentration, factor_y, factor_x):
    x_local, line_total = concentration.shape
    y_local = factor_y.shape[0]
    grid, modes = x_local * px, spectrum.shape[1] * px
    pencil = lax.all_to_all(spectrum, "px", split_axis=2, concat_axis=1, tiled=True)
    lines = pencil.shape[2]
    stacked = pencil.reshape(2 * modes, lines)

    def fill(block, velocity):
        rows = lax.dot_general(
            synth_table(grid, modes, block * x_local, x_local),
            stacked,
            (((0,), (0,)), ((), ())),
            precision=HIGHEST,
            preferred_element_type=jnp.float32,
        )
        return lax.dynamic_update_slice_in_dim(velocity, rows, block * x_local, 0)

    velocity = lax.fori_loop(0, px, fill, jnp.zeros((grid, lines), jnp.float32))
    returned = lax.all_to_all(velocity, "px", split_axis=0, concat_axis=1, tiled=True)
    flux = (returned * concentration).reshape(x_local, y_local, line_total // y_local)
    y_compressed = lax.psum_scatter(
        jnp.einsum("xyz,yr->zxr", flux, factor_y, precision=HIGHEST),
        "py",
        scatter_dimension=0,
        tiled=True,
    )
    terms = jnp.einsum("xs,zxr->zsr", factor_x, y_compressed, precision=HIGHEST)
    return y_compressed, lax.psum_scatter(terms, "px", scatter_dimension=1, tiled=True)


def pack_kernel(planes, groups, blocks_ref, in_ref, *refs):
    outs, turned = refs[:-1], refs[-1]
    turned[...] = in_ref[...].T
    count = turned.shape[0] // planes
    sets = sum(len(g) for g in groups)
    for out, group in zip(outs, groups):
        row = 0
        for j in group:
            for zb in range(planes // sets):
                part = turned[pl.ds(zb * sets + j, count, stride=planes), :]
                if len(out.shape) == 3:
                    out[0, row : row + count, :] = part
                else:
                    out[row : row + count, :] = part
                row += count


def pack_peer(value, block, width, planes, groups):
    rows = value.shape[0]
    sets = sum(len(g) for g in groups)
    shapes = [(width // sets * len(g), rows) for g in groups]
    return pl.pallas_call(
        functools.partial(pack_kernel, planes, groups),
        out_shape=[jax.ShapeDtypeStruct(s, value.dtype) for s in shapes],
        grid_spec=pltpu.PrefetchScalarGridSpec(
            num_scalar_prefetch=1,
            grid=(rows // LANES,),
            in_specs=[pl.BlockSpec((LANES, width), lambda i, b: (i, b[0]))],
            out_specs=[pl.BlockSpec((s[0], LANES), lambda i, b: (0, i)) for s in shapes],
            scratch_shapes=[pltpu.VMEM((width, LANES), value.dtype)],
        ),
        cost_estimate=pl.CostEstimate(flops=0, bytes_accessed=8 * rows * width, transcendentals=0),
        name="pack_peer",
    )(block, value)


def pack_all(value, blocks, width, planes, groups):
    rows, peers = value.shape[0], blocks.shape[0]
    sets = sum(len(g) for g in groups)
    shapes = [(peers, width // sets * len(g), rows) for g in groups]
    return pl.pallas_call(
        functools.partial(pack_kernel, planes, groups),
        out_shape=[jax.ShapeDtypeStruct(s, value.dtype) for s in shapes],
        grid_spec=pltpu.PrefetchScalarGridSpec(
            num_scalar_prefetch=1,
            grid=(peers, rows // LANES),
            in_specs=[pl.BlockSpec((LANES, width), lambda s, i, b: (i, b[s]))],
            out_specs=[pl.BlockSpec((1, s[1], LANES), lambda s, i, b: (s, 0, i)) for s in shapes],
            scratch_shapes=[pltpu.VMEM((width, LANES), value.dtype)],
        ),
        cost_estimate=pl.CostEstimate(
            flops=0, bytes_accessed=8 * rows * width * peers, transcendentals=0
        ),
        name="pack_all",
    )(blocks, value)


def table_kernel(cos_far, sin_far, cos_near, sin_near, out):
    k_local, tiles = cos_far.shape[1], cos_far.shape[2]

    @pl.loop(0, k_local // 8)
    def _(step):
        row = pl.multiple_of(step * 8, 8)
        far_c, far_s = cos_far[0, pl.ds(row, 8), :], sin_far[0, pl.ds(row, 8), :]
        near_c, near_s = cos_near[0, pl.ds(row, 8), :], sin_near[0, pl.ds(row, 8), :]
        for u in range(tiles):
            c, s = far_c[:, u : u + 1], far_s[:, u : u + 1]
            lanes = slice(u * LANES, (u + 1) * LANES)
            out[pl.ds(row, 8), lanes] = c * near_c - s * near_s
            out[pl.ds(pl.multiple_of(k_local + row, 8), 8), lanes] = -(s * near_c + c * near_s)


def build_table(blocks, k_local, x_local):
    peers = blocks.shape[0]
    grid, modes = x_local * peers, k_local * peers
    wave = blocks[:, None] * k_local + jnp.arange(k_local, dtype=jnp.int32)[None, :]
    starts = jnp.arange(x_local // LANES, dtype=jnp.int32) * LANES
    far = (blocks[:, None] * x_local + starts[None, :]).reshape(-1)
    near = jnp.arange(LANES, dtype=jnp.int32)

    def angle(column):
        phase = wave[:, :, None] * column[None, None, :] % grid
        return phase.astype(jnp.float32) * (2.0 * math.pi / grid)

    weight = (jnp.where(wave == 0, 1.0, 2.0) / math.sqrt(modes)).astype(jnp.float32)[:, :, None]
    tables = (
        jnp.cos(angle(far)),
        jnp.sin(angle(far)),
        weight * jnp.cos(angle(near)),
        weight * jnp.sin(angle(near)),
    )
    size = 2 * k_local * peers * grid
    return pl.pallas_call(
        table_kernel,
        out_shape=jax.ShapeDtypeStruct((2 * modes, grid), jnp.float32),
        grid=(peers,),
        in_specs=[pl.BlockSpec((1,) + t.shape[1:], lambda s: (s, 0, 0)) for t in tables],
        out_specs=pl.BlockSpec((2 * k_local, grid), lambda s: (s, 0)),
        cost_estimate=pl.CostEstimate(flops=3 * size, bytes_accessed=4 * size, transcendentals=0),
        name="build_table",
    )(*tables)


def flux_kernel(peers, index_ref, *refs):
    v_refs, (c_ref, fy_ref, out, flux) = refs[:peers], refs[peers:]
    count = c_ref.shape[1]
    for s in range(peers):
        flux[s * count : (s + 1) * count, :] = v_refs[s][...] * c_ref[s]
    out[0] = jnp.dot(
        fy_ref[...], flux[...], precision=HIGHEST, preferred_element_type=jnp.float32
    )


def contract_flux(parts, place, conc, factor, me_y, owners):
    peers, rows, x_local = conc.shape
    count = rows // owners
    rank, y_local = factor.shape
    return pl.pallas_call(
        functools.partial(flux_kernel, peers),
        out_shape=jax.ShapeDtypeStruct((owners, rank, x_local), jnp.float32),
        grid_spec=pltpu.PrefetchScalarGridSpec(
            num_scalar_prefetch=1,
            grid=(owners,),
            in_specs=[
                pl.BlockSpec((count, x_local), lambda t, m: (place * owners + (m[0] ^ t), 0))
                for _ in parts
            ]
            + [
                pl.BlockSpec((peers, count, x_local), lambda t, m: (0, m[0] ^ t, 0)),
                pl.BlockSpec((rank, y_local), lambda t, m: (0, 0)),
            ],
            out_specs=pl.BlockSpec((1, rank, x_local), lambda t, m: (t, 0, 0)),
            scratch_shapes=[pltpu.VMEM((y_local, x_local), jnp.float32)],
        ),
        cost_estimate=pl.CostEstimate(
            flops=2 * owners * rank * y_local * x_local,
            bytes_accessed=8 * peers * rows * x_local,
            transcendentals=0,
        ),
        name="contract_flux",
    )(me_y, *parts, conc, factor)


def aligned_body(px, py, spectrum, concentration, factor_y, factor_x):
    k_local = spectrum.shape[1]
    x_local, line_total = concentration.shape
    y_local, rank = factor_y.shape
    planes = line_total // y_local
    sets = planes // py
    width = line_total // px
    y_peer = y_local // px
    me_x = lax.axis_index("px").astype(jnp.int32)
    me_y = lax.axis_index("py").astype(jnp.int32).reshape(1)
    blocks = me_x ^ jnp.arange(px, dtype=jnp.int32)
    order = far_first(px)
    stacked = spectrum.reshape(2 * k_local, line_total)
    out_groups, back_groups = split_sets(sets)

    packed = {s: pack_peer(stacked, blocks[s : s + 1], width, planes, out_groups) for s in order + [0]}
    arrived = []
    for g in range(len(out_groups)):
        got = {s: exchange(packed[s][g], "px", px, s) for s in order}
        got[0] = packed[0][g]
        arrived.append(got)

    table = build_table(blocks, k_local, x_local)
    conc = pack_all(concentration, blocks, width, planes, [[j] for j in range(sets)])
    factor = jnp.concatenate(
        [lax.dynamic_slice_in_dim(factor_y, blocks[s] * y_peer, y_peer, 0) for s in range(px)], axis=0
    ).T

    rows_set = y_peer * py
    velocity = {}
    for group, got in zip(out_groups, arrived):
        lines = jnp.concatenate([got[s] for s in range(px)], axis=1)
        whole = lax.dot_general(
            lines,
            table,
            (((1,), (0,)), ((), ())),
            precision=lax.Precision.HIGH,
            preferred_element_type=jnp.float32,
        )
        for at, j in enumerate(group):
            velocity[j] = (whole, at)

    y_parts, core_parts = [], []
    for group in back_groups:
        whole, first = velocity[group[0]]
        rows = slice(first * rows_set, (first + len(group)) * rows_set)
        own = whole[rows]
        parts = [None] * px
        parts[0] = own[:, :x_local]
        for s in order:
            parts[s] = exchange(own[:, s * x_local : (s + 1) * x_local], "px", px, s)
        cores = []
        for place, j in enumerate(group):
            sums = contract_flux(parts, place, conc[j], factor, me_y, py)
            total = sums[0]
            for t in range(1, py):
                total = total + exchange(sums[t], "py", py, t)
            y_parts.append(total.T)
            cores.append(
                lax.dot_general(
                    factor_x,
                    total,
                    (((0,), (1,)), ((), ())),
                    precision=HIGHEST,
                    preferred_element_type=jnp.float32,
                )
            )
        s_local = factor_x.shape[1] // px
        terms = jnp.stack(cores).reshape(len(group), px, s_local, rank).transpose(1, 0, 2, 3)
        terms = lax.all_to_all(terms, "px", split_axis=0, concat_axis=0, tiled=True)
        core_parts.append(jnp.sum(terms, axis=0))
    return jnp.stack(y_parts), jnp.concatenate(core_parts, axis=0)


def is_aligned(px, py, spectrum, concentration, factor_y):
    x_local, line_total = concentration.shape[0] // px, concentration.shape[1] // py
    y_local, k_local = factor_y.shape[0] // py, spectrum.shape[1] // px
    planes = line_total // y_local
    return (
        px > 1
        and px & (px - 1) == 0
        and py & (py - 1) == 0
        and planes % py == 0
        and planes % 8 == 0
        and planes // py > 1
        and (line_total // px) % LANES == 0
        and x_local % LANES == 0
        and y_local % (8 * px) == 0
        and k_local * 2 == x_local
        and k_local % 8 == 0
    )


def solution(mesh):
    px, py = mesh.shape["px"], mesh.shape["py"]
    placed = (P(None, "px", "py"), P("px", "py"), P("py", None), P("px", None))
    shard = functools.partial(
        jax.shard_map,
        mesh=mesh,
        in_specs=placed,
        out_specs=(P("py", "px", None), P("py", "px", None)),
        check_vma=False,
    )

    def step(spectrum, concentration, factor_y, factor_x):
        args = (spectrum, concentration, factor_y, factor_x)
        if not is_aligned(px, py, spectrum, concentration, factor_y):
            return shard(functools.partial(general_body, px))(*args)

        def body(*blocks):
            return aligned_body(px, py, *blocks)

        return shard(body)(*args)

    return step
```

```python
import functools
import math

import jax
import jax.numpy as jnp
from jax import lax
from jax.experimental import pallas as pl
from jax.experimental.pallas import tpu as pltpu
from jax.sharding import PartitionSpec as P


HIGHEST = lax.Precision.HIGHEST
LANES = 128


def exchange(value, axis, size, offset):
    return lax.ppermute(value, axis, [(a, a ^ offset) for a in range(size)])


def far_first(peers):
    half = peers // 2
    return list(range(half, peers)) + list(range(1, half))


def split_sets(sets):
    cut = max(1, sets // 2)
    out_groups = [g for g in (list(range(cut)), list(range(cut, sets))) if g]
    back_groups = [list(range(cut))] + [[j] for j in range(cut, sets)]
    return out_groups, back_groups


def synth_table(grid, modes, first_x, block_width):
    wave = lax.broadcasted_iota(jnp.int32, (modes, block_width), 0)
    column = first_x + lax.broadcasted_iota(jnp.int32, (modes, block_width), 1)
    phase = wave * column % grid
    angle = phase.astype(jnp.float32) * (2.0 * math.pi / grid)
    weight = jnp.where(wave == 0, 1.0, 2.0) / math.sqrt(modes)
    return jnp.concatenate([weight * jnp.cos(angle), -weight * jnp.sin(angle)], axis=0)


def general_body(px, spectrum, concentration, factor_y, factor_x):
    x_local, line_total = concentration.shape
    y_local = factor_y.shape[0]
    grid, modes = x_local * px, spectrum.shape[1] * px
    pencil = lax.all_to_all(spectrum, "px", split_axis=2, concat_axis=1, tiled=True)
    lines = pencil.shape[2]
    stacked = pencil.reshape(2 * modes, lines)

    def fill(block, velocity):
        rows = lax.dot_general(
            synth_table(grid, modes, block * x_local, x_local),
            stacked,
            (((0,), (0,)), ((), ())),
            precision=HIGHEST,
            preferred_element_type=jnp.float32,
        )
        return lax.dynamic_update_slice_in_dim(velocity, rows, block * x_local, 0)

    velocity = lax.fori_loop(0, px, fill, jnp.zeros((grid, lines), jnp.float32))
    returned = lax.all_to_all(velocity, "px", split_axis=0, concat_axis=1, tiled=True)
    flux = (returned * concentration).reshape(x_local, y_local, line_total // y_local)
    y_compressed = lax.psum_scatter(
        jnp.einsum("xyz,yr->zxr", flux, factor_y, precision=HIGHEST),
        "py",
        scatter_dimension=0,
        tiled=True,
    )
    terms = jnp.einsum("xs,zxr->zsr", factor_x, y_compressed, precision=HIGHEST)
    return y_compressed, lax.psum_scatter(terms, "px", scatter_dimension=1, tiled=True)


def pack_kernel(planes, groups, blocks_ref, in_ref, *refs):
    outs, turned = refs[:-1], refs[-1]
    turned[...] = in_ref[...].T
    count = turned.shape[0] // planes
    sets = sum(len(g) for g in groups)
    for out, group in zip(outs, groups):
        row = 0
        for j in group:
            for zb in range(planes // sets):
                part = turned[pl.ds(zb * sets + j, count, stride=planes), :]
                if len(out.shape) == 3:
                    out[0, row : row + count, :] = part
                else:
                    out[row : row + count, :] = part
                row += count


def pack_peer(value, block, width, planes, groups):
    rows = value.shape[0]
    sets = sum(len(g) for g in groups)
    shapes = [(width // sets * len(g), rows) for g in groups]
    return pl.pallas_call(
        functools.partial(pack_kernel, planes, groups),
        out_shape=[jax.ShapeDtypeStruct(s, value.dtype) for s in shapes],
        grid_spec=pltpu.PrefetchScalarGridSpec(
            num_scalar_prefetch=1,
            grid=(rows // LANES,),
            in_specs=[pl.BlockSpec((LANES, width), lambda i, b: (i, b[0]))],
            out_specs=[pl.BlockSpec((s[0], LANES), lambda i, b: (0, i)) for s in shapes],
            scratch_shapes=[pltpu.VMEM((width, LANES), value.dtype)],
        ),
        cost_estimate=pl.CostEstimate(flops=0, bytes_accessed=8 * rows * width, transcendentals=0),
        name="pack_peer",
    )(block, value)


def pack_all(value, blocks, width, planes, groups):
    rows, peers = value.shape[0], blocks.shape[0]
    sets = sum(len(g) for g in groups)
    shapes = [(peers, width // sets * len(g), rows) for g in groups]
    return pl.pallas_call(
        functools.partial(pack_kernel, planes, groups),
        out_shape=[jax.ShapeDtypeStruct(s, value.dtype) for s in shapes],
        grid_spec=pltpu.PrefetchScalarGridSpec(
            num_scalar_prefetch=1,
            grid=(peers, rows // LANES),
            in_specs=[pl.BlockSpec((LANES, width), lambda s, i, b: (i, b[s]))],
            out_specs=[pl.BlockSpec((1, s[1], LANES), lambda s, i, b: (s, 0, i)) for s in shapes],
            scratch_shapes=[pltpu.VMEM((width, LANES), value.dtype)],
        ),
        cost_estimate=pl.CostEstimate(
            flops=0, bytes_accessed=8 * rows * width * peers, transcendentals=0
        ),
        name="pack_all",
    )(blocks, value)


def table_kernel(cos_far, sin_far, cos_near, sin_near, out):
    k_local, tiles = cos_far.shape[1], cos_far.shape[2]

    @pl.loop(0, k_local // 8)
    def _(step):
        row = pl.multiple_of(step * 8, 8)
        far_c, far_s = cos_far[0, pl.ds(row, 8), :], sin_far[0, pl.ds(row, 8), :]
        near_c, near_s = cos_near[0, pl.ds(row, 8), :], sin_near[0, pl.ds(row, 8), :]
        for u in range(tiles):
            c, s = far_c[:, u : u + 1], far_s[:, u : u + 1]
            lanes = slice(u * LANES, (u + 1) * LANES)
            out[pl.ds(row, 8), lanes] = c * near_c - s * near_s
            out[pl.ds(pl.multiple_of(k_local + row, 8), 8), lanes] = -(s * near_c + c * near_s)


def build_table(blocks, k_local, x_local):
    peers = blocks.shape[0]
    grid, modes = x_local * peers, k_local * peers
    wave = blocks[:, None] * k_local + jnp.arange(k_local, dtype=jnp.int32)[None, :]
    starts = jnp.arange(x_local // LANES, dtype=jnp.int32) * LANES
    far = (blocks[:, None] * x_local + starts[None, :]).reshape(-1)
    near = jnp.arange(LANES, dtype=jnp.int32)

    def angle(column):
        phase = wave[:, :, None] * column[None, None, :] % grid
        return phase.astype(jnp.float32) * (2.0 * math.pi / grid)

    weight = (jnp.where(wave == 0, 1.0, 2.0) / math.sqrt(modes)).astype(jnp.float32)[:, :, None]
    tables = (
        jnp.cos(angle(far)),
        jnp.sin(angle(far)),
        weight * jnp.cos(angle(near)),
        weight * jnp.sin(angle(near)),
    )
    size = 2 * k_local * peers * grid
    return pl.pallas_call(
        table_kernel,
        out_shape=jax.ShapeDtypeStruct((2 * modes, grid), jnp.float32),
        grid=(peers,),
        in_specs=[pl.BlockSpec((1,) + t.shape[1:], lambda s: (s, 0, 0)) for t in tables],
        out_specs=pl.BlockSpec((2 * k_local, grid), lambda s: (s, 0)),
        cost_estimate=pl.CostEstimate(flops=3 * size, bytes_accessed=4 * size, transcendentals=0),
        name="build_table",
    )(*tables)


def flux_kernel(peers, index_ref, *refs):
    v_refs, (c_ref, fy_ref, *outs, flux) = refs[:peers], refs[peers:]
    count = c_ref.shape[1]
    for s in range(peers):
        flux[s * count : (s + 1) * count, :] = v_refs[s][...] * c_ref[s]
    sums = jnp.dot(fy_ref[...], flux[...], precision=HIGHEST, preferred_element_type=jnp.float32)
    for t, out in enumerate(outs):

        @pl.when(pl.program_id(0) == t)
        def _(out=out):
            out[...] = sums


def contract_flux(parts, place, conc, factor, me_y, owners):
    peers, rows, x_local = conc.shape
    count = rows // owners
    rank, y_local = factor.shape
    return pl.pallas_call(
        functools.partial(flux_kernel, peers),
        out_shape=[jax.ShapeDtypeStruct((rank, x_local), jnp.float32)] * owners,
        grid_spec=pltpu.PrefetchScalarGridSpec(
            num_scalar_prefetch=1,
            grid=(owners,),
            in_specs=[
                pl.BlockSpec((count, x_local), lambda t, m: (place * owners + (m[0] ^ t), 0))
                for _ in parts
            ]
            + [
                pl.BlockSpec((peers, count, x_local), lambda t, m: (0, m[0] ^ t, 0)),
                pl.BlockSpec((rank, y_local), lambda t, m: (0, 0)),
            ],
            out_specs=[pl.BlockSpec((rank, x_local), lambda t, m: (0, 0))] * owners,
            scratch_shapes=[pltpu.VMEM((y_local, x_local), jnp.float32)],
        ),
        cost_estimate=pl.CostEstimate(
            flops=2 * owners * rank * y_local * x_local,
            bytes_accessed=8 * peers * rows * x_local,
            transcendentals=0,
        ),
        name="contract_flux",
    )(me_y, *parts, conc, factor)


def aligned_body(px, py, spectrum, concentration, factor_y, factor_x):
    k_local = spectrum.shape[1]
    x_local, line_total = concentration.shape
    y_local, _ = factor_y.shape
    planes = line_total // y_local
    sets = planes // py
    width = line_total // px
    y_peer = y_local // px
    me_x = lax.axis_index("px").astype(jnp.int32)
    me_y = lax.axis_index("py").astype(jnp.int32).reshape(1)
    blocks = me_x ^ jnp.arange(px, dtype=jnp.int32)
    order = far_first(px)
    stacked = spectrum.reshape(2 * k_local, line_total)
    out_groups, back_groups = split_sets(sets)

    packed = {s: pack_peer(stacked, blocks[s : s + 1], width, planes, out_groups) for s in order + [0]}
    arrived = []
    for g in range(len(out_groups)):
        got = {s: exchange(packed[s][g], "px", px, s) for s in order}
        got[0] = packed[0][g]
        arrived.append(got)

    table = build_table(blocks, k_local, x_local)
    conc = pack_all(concentration, blocks, width, planes, [[j] for j in range(sets)])
    factor = jnp.concatenate(
        [lax.dynamic_slice_in_dim(factor_y, blocks[s] * y_peer, y_peer, 0) for s in range(px)], axis=0
    ).T

    rows_set = y_peer * py
    velocity = {}
    for group, got in zip(out_groups, arrived):
        lines = jnp.concatenate([got[s] for s in range(px)], axis=1)
        whole = lax.dot_general(
            lines,
            table,
            (((1,), (0,)), ((), ())),
            precision=lax.Precision.HIGH,
            preferred_element_type=jnp.float32,
        )
        for at, j in enumerate(group):
            velocity[j] = (whole, at)

    s_local = factor_x.shape[1] // px
    factor_s = jnp.concatenate(
        [lax.dynamic_slice_in_dim(factor_x, blocks[s] * s_local, s_local, 1) for s in range(px)], axis=1
    )
    y_parts, cores, core_parts = [], [], []
    for g, group in enumerate(back_groups):
        whole, first = velocity[group[0]]
        rows = slice(first * rows_set, (first + len(group)) * rows_set)
        own = whole[rows]
        parts = [None] * px
        parts[0] = own[:, :x_local]
        for s in order:
            parts[s] = exchange(own[:, s * x_local : (s + 1) * x_local], "px", px, s)
        for place, j in enumerate(group):
            sums = contract_flux(parts, place, conc[j], factor, me_y, py)
            total = sums[0]
            for t in range(1, py):
                total = total + exchange(sums[t], "py", py, t)
            y_parts.append(total.T)
            cores.append(
                lax.dot_general(
                    factor_s,
                    total,
                    (((0,), (1,)), ((), ())),
                    precision=HIGHEST,
                    preferred_element_type=jnp.float32,
                )
            )
        if g >= len(back_groups) - 2:
            terms = [
                jnp.stack([c[s * s_local : (s + 1) * s_local] for c in cores]) for s in range(px)
            ]
            summed = terms[0]
            for s in order:
                summed = summed + exchange(terms[s], "px", px, s)
            core_parts.append(summed)
            cores = []
    return jnp.stack(y_parts), jnp.concatenate(core_parts, axis=0)


def is_aligned(px, py, spectrum, concentration, factor_y):
    x_local, line_total = concentration.shape[0] // px, concentration.shape[1] // py
    y_local, k_local = factor_y.shape[0] // py, spectrum.shape[1] // px
    planes = line_total // y_local
    return (
        px > 1
        and px & (px - 1) == 0
        and py & (py - 1) == 0
        and planes % py == 0
        and planes % 8 == 0
        and planes // py > 1
        and (line_total // px) % LANES == 0
        and x_local % LANES == 0
        and y_local % (8 * px) == 0
        and k_local * 2 == x_local
        and k_local % 8 == 0
    )


def solution(mesh):
    px, py = mesh.shape["px"], mesh.shape["py"]
    placed = (P(None, "px", "py"), P("px", "py"), P("py", None), P("px", None))
    shard = functools.partial(
        jax.shard_map,
        mesh=mesh,
        in_specs=placed,
        out_specs=(P("py", "px", None), P("py", "px", None)),
        check_vma=False,
    )

    def step(spectrum, concentration, factor_y, factor_x):
        args = (spectrum, concentration, factor_y, factor_x)
        if not is_aligned(px, py, spectrum, concentration, factor_y):
            return shard(functools.partial(general_body, px))(*args)

        def body(*blocks):
            return aligned_body(px, py, *blocks)

        return shard(body)(*args)

    return step
```

```python
import functools
import math

import jax
import jax.numpy as jnp
from jax import lax
from jax.experimental import pallas as pl
from jax.experimental.pallas import tpu as pltpu
from jax.sharding import PartitionSpec as P


HIGHEST = lax.Precision.HIGHEST
LANES = 128


def exchange(value, axis, size, offset):
    return lax.ppermute(value, axis, [(a, a ^ offset) for a in range(size)])


def far_first(peers):
    half = peers // 2
    return list(range(half, peers)) + list(range(1, half))


def split_sets(sets):
    cut = max(1, sets // 2)
    out_groups = [g for g in (list(range(cut)), list(range(cut, sets))) if g]
    back_groups = [list(range(cut))] + [[j] for j in range(cut, sets)]
    return out_groups, back_groups


def synth_table(grid, modes, first_x, block_width):
    wave = lax.broadcasted_iota(jnp.int32, (modes, block_width), 0)
    column = first_x + lax.broadcasted_iota(jnp.int32, (modes, block_width), 1)
    phase = wave * column % grid
    angle = phase.astype(jnp.float32) * (2.0 * math.pi / grid)
    weight = jnp.where(wave == 0, 1.0, 2.0) / math.sqrt(modes)
    return jnp.concatenate([weight * jnp.cos(angle), -weight * jnp.sin(angle)], axis=0)


def general_body(px, spectrum, concentration, factor_y, factor_x):
    x_local, line_total = concentration.shape
    y_local = factor_y.shape[0]
    grid, modes = x_local * px, spectrum.shape[1] * px
    pencil = lax.all_to_all(spectrum, "px", split_axis=2, concat_axis=1, tiled=True)
    lines = pencil.shape[2]
    stacked = pencil.reshape(2 * modes, lines)

    def fill(block, velocity):
        rows = lax.dot_general(
            synth_table(grid, modes, block * x_local, x_local),
            stacked,
            (((0,), (0,)), ((), ())),
            precision=HIGHEST,
            preferred_element_type=jnp.float32,
        )
        return lax.dynamic_update_slice_in_dim(velocity, rows, block * x_local, 0)

    velocity = lax.fori_loop(0, px, fill, jnp.zeros((grid, lines), jnp.float32))
    returned = lax.all_to_all(velocity, "px", split_axis=0, concat_axis=1, tiled=True)
    flux = (returned * concentration).reshape(x_local, y_local, line_total // y_local)
    y_compressed = lax.psum_scatter(
        jnp.einsum("xyz,yr->zxr", flux, factor_y, precision=HIGHEST),
        "py",
        scatter_dimension=0,
        tiled=True,
    )
    terms = jnp.einsum("xs,zxr->zsr", factor_x, y_compressed, precision=HIGHEST)
    return y_compressed, lax.psum_scatter(terms, "px", scatter_dimension=1, tiled=True)


def pack_kernel(planes, groups, blocks_ref, in_ref, *refs):
    outs, turned = refs[:-1], refs[-1]
    turned[...] = in_ref[...].T
    count = turned.shape[0] // planes
    sets = sum(len(g) for g in groups)
    for out, group in zip(outs, groups):
        row = 0
        for j in group:
            for zb in range(planes // sets):
                part = turned[pl.ds(zb * sets + j, count, stride=planes), :]
                if len(out.shape) == 3:
                    out[0, row : row + count, :] = part
                else:
                    out[row : row + count, :] = part
                row += count


def pack_peer(value, block, width, planes, groups):
    rows = value.shape[0]
    sets = sum(len(g) for g in groups)
    shapes = [(width // sets * len(g), rows) for g in groups]
    return pl.pallas_call(
        functools.partial(pack_kernel, planes, groups),
        out_shape=[jax.ShapeDtypeStruct(s, value.dtype) for s in shapes],
        grid_spec=pltpu.PrefetchScalarGridSpec(
            num_scalar_prefetch=1,
            grid=(rows // LANES,),
            in_specs=[pl.BlockSpec((LANES, width), lambda i, b: (i, b[0]))],
            out_specs=[pl.BlockSpec((s[0], LANES), lambda i, b: (0, i)) for s in shapes],
            scratch_shapes=[pltpu.VMEM((width, LANES), value.dtype)],
        ),
        cost_estimate=pl.CostEstimate(flops=0, bytes_accessed=8 * rows * width, transcendentals=0),
        name="pack_peer",
    )(block, value)


def pack_all(value, blocks, width, planes, groups):
    rows, peers = value.shape[0], blocks.shape[0]
    sets = sum(len(g) for g in groups)
    shapes = [(peers, width // sets * len(g), rows) for g in groups]
    return pl.pallas_call(
        functools.partial(pack_kernel, planes, groups),
        out_shape=[jax.ShapeDtypeStruct(s, value.dtype) for s in shapes],
        grid_spec=pltpu.PrefetchScalarGridSpec(
            num_scalar_prefetch=1,
            grid=(peers, rows // LANES),
            in_specs=[pl.BlockSpec((LANES, width), lambda s, i, b: (i, b[s]))],
            out_specs=[pl.BlockSpec((1, s[1], LANES), lambda s, i, b: (s, 0, i)) for s in shapes],
            scratch_shapes=[pltpu.VMEM((width, LANES), value.dtype)],
        ),
        cost_estimate=pl.CostEstimate(
            flops=0, bytes_accessed=8 * rows * width * peers, transcendentals=0
        ),
        name="pack_all",
    )(blocks, value)


def table_kernel(cos_far, sin_far, cos_near, sin_near, out):
    k_local, tiles = cos_far.shape[1], cos_far.shape[2]

    @pl.loop(0, k_local // 8)
    def _(step):
        row = pl.multiple_of(step * 8, 8)
        far_c, far_s = cos_far[0, pl.ds(row, 8), :], sin_far[0, pl.ds(row, 8), :]
        near_c, near_s = cos_near[0, pl.ds(row, 8), :], sin_near[0, pl.ds(row, 8), :]
        for u in range(tiles):
            c, s = far_c[:, u : u + 1], far_s[:, u : u + 1]
            lanes = slice(u * LANES, (u + 1) * LANES)
            out[pl.ds(row, 8), lanes] = c * near_c - s * near_s
            out[pl.ds(pl.multiple_of(k_local + row, 8), 8), lanes] = -(s * near_c + c * near_s)


def build_table(blocks, k_local, x_local):
    peers = blocks.shape[0]
    grid, modes = x_local * peers, k_local * peers
    wave = blocks[:, None] * k_local + jnp.arange(k_local, dtype=jnp.int32)[None, :]
    starts = jnp.arange(x_local // LANES, dtype=jnp.int32) * LANES
    far = (blocks[:, None] * x_local + starts[None, :]).reshape(-1)
    near = jnp.arange(LANES, dtype=jnp.int32)

    def angle(column):
        phase = wave[:, :, None] * column[None, None, :] % grid
        return phase.astype(jnp.float32) * (2.0 * math.pi / grid)

    weight = (jnp.where(wave == 0, 1.0, 2.0) / math.sqrt(modes)).astype(jnp.float32)[:, :, None]
    tables = (
        jnp.cos(angle(far)),
        jnp.sin(angle(far)),
        weight * jnp.cos(angle(near)),
        weight * jnp.sin(angle(near)),
    )
    size = 2 * k_local * peers * grid
    return pl.pallas_call(
        table_kernel,
        out_shape=jax.ShapeDtypeStruct((2 * modes, grid), jnp.float32),
        grid=(peers,),
        in_specs=[pl.BlockSpec((1,) + t.shape[1:], lambda s: (s, 0, 0)) for t in tables],
        out_specs=pl.BlockSpec((2 * k_local, grid), lambda s: (s, 0)),
        cost_estimate=pl.CostEstimate(flops=3 * size, bytes_accessed=4 * size, transcendentals=0),
        name="build_table",
    )(*tables)


def flux_kernel(peers, index_ref, *refs):
    v_refs, (c_ref, fy_ref, *outs, flux) = refs[:peers], refs[peers:]
    count = c_ref.shape[1]
    for s in range(peers):
        flux[s * count : (s + 1) * count, :] = v_refs[s][...] * c_ref[s]
    sums = jnp.dot(fy_ref[...], flux[...], precision=HIGHEST, preferred_element_type=jnp.float32)
    for t, out in enumerate(outs):

        @pl.when(pl.program_id(0) == t)
        def _(out=out):
            out[...] = sums


def contract_flux(parts, place, conc, factor, me_y, owners):
    peers, rows, x_local = conc.shape
    count = rows // owners
    rank, y_local = factor.shape
    return pl.pallas_call(
        functools.partial(flux_kernel, peers),
        out_shape=[jax.ShapeDtypeStruct((rank, x_local), jnp.float32)] * owners,
        grid_spec=pltpu.PrefetchScalarGridSpec(
            num_scalar_prefetch=1,
            grid=(owners,),
            in_specs=[
                pl.BlockSpec((count, x_local), lambda t, m: (place * owners + (m[0] ^ t), 0))
                for _ in parts
            ]
            + [
                pl.BlockSpec((peers, count, x_local), lambda t, m: (0, m[0] ^ t, 0)),
                pl.BlockSpec((rank, y_local), lambda t, m: (0, 0)),
            ],
            out_specs=[pl.BlockSpec((rank, x_local), lambda t, m: (0, 0))] * owners,
            scratch_shapes=[pltpu.VMEM((y_local, x_local), jnp.float32)],
        ),
        cost_estimate=pl.CostEstimate(
            flops=2 * owners * rank * y_local * x_local,
            bytes_accessed=8 * peers * rows * x_local,
            transcendentals=0,
        ),
        name="contract_flux",
    )(me_y, *parts, conc, factor)


def aligned_body(px, py, spectrum, concentration, factor_y, factor_x):
    k_local = spectrum.shape[1]
    x_local, line_total = concentration.shape
    y_local, rank = factor_y.shape
    planes = line_total // y_local
    sets = planes // py
    width = line_total // px
    y_peer = y_local // px
    me_x = lax.axis_index("px").astype(jnp.int32)
    me_y = lax.axis_index("py").astype(jnp.int32).reshape(1)
    blocks = me_x ^ jnp.arange(px, dtype=jnp.int32)
    order = far_first(px)
    stacked = spectrum.reshape(2 * k_local, line_total)
    out_groups, back_groups = split_sets(sets)

    packed = {s: pack_peer(stacked, blocks[s : s + 1], width, planes, out_groups) for s in order + [0]}
    arrived = []
    for g in range(len(out_groups)):
        got = {s: exchange(packed[s][g], "px", px, s) for s in order}
        got[0] = packed[0][g]
        arrived.append(got)

    table = build_table(blocks, k_local, x_local)
    conc = pack_all(concentration, blocks, width, planes, [[j] for j in range(sets)])
    factor = jnp.concatenate(
        [lax.dynamic_slice_in_dim(factor_y, blocks[s] * y_peer, y_peer, 0) for s in range(px)], axis=0
    ).T

    rows_set = y_peer * py
    velocity = {}
    for group, got in zip(out_groups, arrived):
        lines = jnp.concatenate([got[s] for s in range(px)], axis=1)
        whole = lax.dot_general(
            lines,
            table,
            (((1,), (0,)), ((), ())),
            precision=lax.Precision.HIGH,
            preferred_element_type=jnp.float32,
        )
        for at, j in enumerate(group):
            velocity[j] = (whole, at)

    s_local = factor_x.shape[1] // px
    y_parts, cores, core_parts = [], [], []
    for g, group in enumerate(back_groups):
        whole, first = velocity[group[0]]
        rows = slice(first * rows_set, (first + len(group)) * rows_set)
        own = whole[rows]
        parts = [None] * px
        parts[0] = own[:, :x_local]
        for s in order:
            parts[s] = exchange(own[:, s * x_local : (s + 1) * x_local], "px", px, s)
        for place, j in enumerate(group):
            sums = contract_flux(parts, place, conc[j], factor, me_y, py)
            total = sums[0]
            for t in range(1, py):
                total = total + exchange(sums[t], "py", py, t)
            y_parts.append(total.T)
            cores.append(
                lax.dot_general(
                    factor_x,
                    total,
                    (((0,), (1,)), ((), ())),
                    precision=HIGHEST,
                    preferred_element_type=jnp.float32,
                )
            )
        if g in (0, len(back_groups) - 1):
            terms = jnp.stack(cores).reshape(len(cores), px, s_local, rank).transpose(1, 0, 2, 3)
            terms = lax.all_to_all(terms, "px", split_axis=0, concat_axis=0, tiled=True)
            core_parts.append(jnp.sum(terms, axis=0))
            cores = []
    return jnp.stack(y_parts), jnp.concatenate(core_parts, axis=0)


def is_aligned(px, py, spectrum, concentration, factor_y):
    x_local, line_total = concentration.shape[0] // px, concentration.shape[1] // py
    y_local, k_local = factor_y.shape[0] // py, spectrum.shape[1] // px
    planes = line_total // y_local
    return (
        px > 1
        and px & (px - 1) == 0
        and py & (py - 1) == 0
        and planes % py == 0
        and planes % 8 == 0
        and planes // py > 1
        and (line_total // px) % LANES == 0
        and x_local % LANES == 0
        and y_local % (8 * px) == 0
        and k_local * 2 == x_local
        and k_local % 8 == 0
    )


def solution(mesh):
    px, py = mesh.shape["px"], mesh.shape["py"]
    placed = (P(None, "px", "py"), P("px", "py"), P("py", None), P("px", None))
    shard = functools.partial(
        jax.shard_map,
        mesh=mesh,
        in_specs=placed,
        out_specs=(P("py", "px", None), P("py", "px", None)),
        check_vma=False,
    )

    def step(spectrum, concentration, factor_y, factor_x):
        args = (spectrum, concentration, factor_y, factor_x)
        if not is_aligned(px, py, spectrum, concentration, factor_y):
            return shard(functools.partial(general_body, px))(*args)

        def body(*blocks):
            return aligned_body(px, py, *blocks)

        return shard(body)(*args)

    return step
```
